512 devices in a mesh: seq: 128 (over z, y, core), tp: 4 (over x).
Axes of the slice: x: 4, y: 8, z: 8, core: 2. Of those that a mesh axis runs over, the one named last changes fastest.
Arguments:
- tokens: bfloat16 [32768, 1536], P('seq', 'tp'), may hold values from -6 to 6
- norm_gain: float32 [1536], replicated, may hold values from 0.1 to 1.9
- query_weight: bfloat16 [1536, 1536], P(None, 'tp'), may hold values from -0.15625 to 0.15625
- query_bias: float32 [1536], P('tp'), may hold values from -10 to 10
- kv_weight: bfloat16 [1536, 512], P(None, 'tp'), may hold values from -0.15625 to 0.15625
- kv_bias: float32 [512], P('tp'), may hold values from -3 to 3
- out_weight: bfloat16 [1536, 1536], P('tp'), may hold values from -0.625 to 0.625
- shared_slot: bfloat16 [32768, 512], P('seq'), may hold values from -6 to 6
- shared_len: int32 [5], replicated, may hold values from 1 to 256, as said below
- shared_owner: int32 [5], replicated, may hold values from 0 to 127, as said below
- hist_pool: bfloat16 [2048, 64, 512], P('seq'), may hold values from -6 to 6
- hist_pages: int32 [128, 16], P('seq'), may hold values from 0 to 15, each once within a row
- hist_len: int32 [128, 4], P('seq'), may hold values from 1 to 256, as said below
- req_len: int32 [128, 4], P('seq'), may hold values from 1 to 128, 256 in all within a row
- req_offset: int32 [128, 4], P('seq'), may hold values from 0 to 3, each once within a row
- req_parent: int32 [128, 4], P('seq'), may hold values from 0 to 3
Outputs:
- hidden: bfloat16 [32768, 1536], P('seq', 'tp')
- new_cache: bfloat16 [32768, 512], P('seq', 'tp')
The draws below stay inside these ranges and needn't reach their ends.
Inputs may be any that keep to these rules, and one draw needn't show every extreme that they name: `shared_owner`: all different; entry 0 is the root's. `shared_len`: some entry equals 256. `hist_len`: some request's history has exactly 256 rows.
All inputs are finite; a program needn't handle non-finite values.
Results may differ from the reference program's by a relative error of at most 0.017.
Values may be sent and summed in bfloat16 or wider, within the bound.
No kernel may reach another device: no remote copies, remote signals or barrier semaphores. Data moves between devices by JAX's collectives and lax.ppermute only.
A program may use at most 64 MiB of HBM per device.

```python
import math
import jax
import jax.numpy as jnp
import numpy as np
from jax import lax

D = 1536
HEADS = 12
KV_HEADS = 2
HEAD_DIM = 128
TOK_DEV = 256
REQ_DEV = 4
NODES1 = 4
SHARED_LEN = 256
PAGE = 64
PAGES = 4
MOST = 128
HIST_CAP = 256
SEQ_DEVS = 128
TOKENS = 32768
N_TP = 4


def draw_shared_len(key, part):
    node_total = NODES1 + 1
    drawn = jax.random.randint(key, (node_total,), 1, SHARED_LEN + 1)
    chosen = jax.random.randint(jax.random.fold_in(key, 11), (), 0, node_total)
    return jnp.where(jnp.arange(node_total) == chosen, SHARED_LEN, drawn).astype(jnp.int32)


def draw_shared_owner(key, part):
    middle = 1 + jax.random.permutation(key, SEQ_DEVS - 2)[:NODES1 - 1]
    ends = jnp.array([0, SEQ_DEVS - 1], dtype=jnp.int32)
    candidates = jnp.concatenate([ends, middle.astype(jnp.int32)])
    order = jax.random.permutation(jax.random.fold_in(key, 17), NODES1 + 1)
    return candidates[order].astype(jnp.int32)


def draw_hist_len(key, part):
    drawn = jax.random.randint(key, (SEQ_DEVS, REQ_DEV), 1, HIST_CAP + 1)
    chosen = jax.random.randint(jax.random.fold_in(key, 13), (), 0, SEQ_DEVS * REQ_DEV)
    flat_index = jnp.arange(SEQ_DEVS * REQ_DEV).reshape(SEQ_DEVS, REQ_DEV)
    return jnp.where(flat_index == chosen, HIST_CAP, drawn).astype(jnp.int32)


def draw_query_bias(key, part):
    base = jax.random.fold_in(key, 201)
    return jnp.clip(0.5 * jax.random.normal(base, (HEADS * HEAD_DIM,), jnp.float32), -3.0, 3.0)


def draw_shared_slot(key, part):
    base = jax.random.fold_in(key, 301)
    row_total = SEQ_DEVS * SHARED_LEN
    return jnp.clip(jax.random.normal(base, (row_total, KV_HEADS * 2 * HEAD_DIM), jnp.float32), -6.0, 6.0).astype(jnp.bfloat16)


def draw_hist_pool(key, part):
    base = jax.random.fold_in(key, 401)
    row_total = SEQ_DEVS * REQ_DEV * PAGES * PAGE
    drawn = jnp.clip(jax.random.normal(base, (row_total, KV_HEADS * 2 * HEAD_DIM), jnp.float32), -6.0, 6.0)
    return drawn.reshape(SEQ_DEVS * REQ_DEV * PAGES, PAGE, KV_HEADS * 2 * HEAD_DIM).astype(jnp.bfloat16)


def touch_ends(values, rng, low, high):
    longest = values.shape.index(max(values.shape))
    spots = []
    for shift in (0, 1):
        where = [jax.random.randint(jax.random.fold_in(rng, axis), (), 0, length) for axis, length in enumerate(values.shape)]
        where[longest] = (where[longest] + shift) % values.shape[longest]
        spots.append(tuple(where))
    return values.at[spots[0]].set(low).at[spots[1]].set(high)


def steps_of(rng, shape, split, smallest, largest):
    level = 1.0
    for axis_at, shards_of in split:
        draws = jax.random.uniform(jax.random.fold_in(jax.random.fold_in(rng, 6), axis_at), (shards_of,), jnp.float32, smallest / len(split), largest / len(split))
        level = level * jnp.repeat(jnp.exp(draws), shape[axis_at] // shards_of).reshape((-1,) + (1,) * (len(shape) - 1 - axis_at))
    return level


def split_up(number_of, total, bound, slope):
    weights = [(1 << 20) // math.isqrt(standing ** slope) + 1 for standing in range(2, number_of + 1)]
    rest, counts = total - bound - (number_of - 1), [1] * (number_of - 1)
    while rest > 0:
        movable = [i for i in range(number_of - 1) if counts[i] < bound]
        pool, remaining = sum([weights[i] for i in movable]), rest
        for i in movable:
            addition = min(bound - counts[i], max(1, remaining * weights[i] // pool), rest)
            counts[i] = counts[i] + addition
            rest = rest - addition
    return np.array([bound] + counts)


def uneven(key, amount, total, limit, slope):
    if amount == 2:
        one = jax.random.randint(key, (), max(1, total - limit), min(limit, total - 1) + 1)
        return jnp.stack([one, total - one])
    lengths = jnp.asarray(split_up(amount, total, limit, slope), jnp.int32)
    twos = (amount - 1) // 2
    source_of, receiver = lengths[1:1 + 2 * twos:2], lengths[2:2 + 2 * twos:2]
    slack = jnp.minimum(source_of - 1, limit - receiver)
    moved = jax.random.randint(jax.random.fold_in(key, 1), (twos,), 0, 1 << 20) % (slack + 1)
    lengths = lengths.at[1:1 + 2 * twos:2].set(source_of - moved).at[2:2 + 2 * twos:2].set(receiver + moved)
    return lengths[jax.random.permutation(jax.random.fold_in(key, 2), amount)]


def scatter_about(stream_key, shape, scale, reach, shards=(), held_as=jnp.bfloat16):
    values = scale * jax.random.normal(stream_key, shape, jnp.float32)
    if shards:
        values = values * steps_of(stream_key, shape, shards, -0.22, 0.18)
    return jnp.clip(values, -reach, reach).astype(held_as)


def setup_inputs(seed: int = 0) -> dict:
    arg_keys = jax.random.split(jax.random.key(seed), 17)
    return {
        "tokens": scatter_about(arg_keys[0], (TOKENS, D), 1.0, 6.0, ((0, 128), (1, 4))),
        "norm_gain": jnp.clip(1.0 + 0.18 * jax.random.normal(arg_keys[1], (D,), jnp.float32), 0.1, 1.9),
        "query_weight": scatter_about(arg_keys[2], (D, HEADS * HEAD_DIM), D ** -0.5, 0.15625, ((1, 4),)),
        "query_bias": draw_query_bias(jax.random.fold_in(arg_keys[16], 71), 0),
        "kv_weight": scatter_about(arg_keys[4], (D, KV_HEADS * 2 * HEAD_DIM), D ** -0.5, 0.15625, ((1, 4),)),
        "kv_bias": scatter_about(arg_keys[5], (KV_HEADS * 2 * HEAD_DIM,), 0.5, 3.0, ((0, 4),), jnp.float32),
        "out_weight": scatter_about(arg_keys[6], (HEADS * HEAD_DIM, D), (HEADS * HEAD_DIM // 16) ** -0.5, 0.625, ((0, 4),)),
        "shared_slot": draw_shared_slot(jax.random.fold_in(arg_keys[16], 71), 0),
        "shared_len": draw_shared_len(jax.random.fold_in(arg_keys[16], 71), 0),
        "shared_owner": draw_shared_owner(jax.random.fold_in(arg_keys[16], 71), 0),
        "hist_pool": draw_hist_pool(jax.random.fold_in(arg_keys[16], 71), 0),
        "hist_pages": jax.vmap(lambda own: jax.random.permutation(own, REQ_DEV * PAGES))(jax.random.split(arg_keys[11], SEQ_DEVS)).reshape((SEQ_DEVS, REQ_DEV * PAGES)).astype(jnp.int32),
        "hist_len": draw_hist_len(jax.random.fold_in(arg_keys[16], 71), 0),
        "req_len": jax.vmap(lambda own: uneven(own, REQ_DEV, TOK_DEV, MOST, 2))(jax.random.split(arg_keys[13], SEQ_DEVS)).reshape((SEQ_DEVS, REQ_DEV)).astype(jnp.int32),
        "req_offset": jax.vmap(lambda own: jax.random.permutation(own, REQ_DEV))(jax.random.split(arg_keys[14], SEQ_DEVS)).reshape((SEQ_DEVS, REQ_DEV)).astype(jnp.int32),
        "req_parent": touch_ends(jax.random.randint(arg_keys[15], (SEQ_DEVS, REQ_DEV), 0, NODES1), jax.random.fold_in(arg_keys[15], 1), 0, NODES1 - 1).astype(jnp.int32),
    }


norm_eps = 1e-06
rope_base = 1000000.0
neighbour_steps = (-2, -1, 1, 2)
masked_score = -1e+30

def request_layout(req_len, req_parent, hist_len, shared_len, row_count):
    request_end = jnp.cumsum(req_len, axis=1).astype(jnp.int32)
    request_start = (request_end - req_len).astype(jnp.int32)
    row_index = jnp.arange(row_count, dtype=jnp.int32)
    row_request = lax.optimization_barrier(jnp.sum((row_index[None, :, None] >= request_end[:, None, :]).astype(jnp.int32), axis=2)).astype(jnp.int32)
    slot_numbers = jnp.arange(req_len.shape[1], dtype=jnp.int32)
    chosen = row_request[:, :, None] == slot_numbers[None, None, :]

    def lookup(table):
        return lax.optimization_barrier(jnp.sum(jnp.where(chosen, table[:, None, :], 0), axis=2)).astype(jnp.int32)
    row_offset = row_index[None, :] - lookup(request_start)
    row_parent = lookup(req_parent)
    node_numbers = jnp.arange(shared_len.shape[0] - 1, dtype=jnp.int32)
    parent_length = lax.optimization_barrier(jnp.sum(jnp.where(row_parent[:, :, None] == node_numbers, shared_len[1:], 0), axis=2)).astype(jnp.int32)
    position = shared_len[0] + parent_length + lookup(hist_len) + row_offset
    return (row_request, row_parent, position.astype(jnp.int32))

def rotate(values, position):
    half_dim = values.shape[-1] // 2
    frequency = rope_base ** (-2.0 * jnp.arange(half_dim, dtype=jnp.float32) / values.shape[-1])
    angle = position.astype(jnp.float32)[:, None, None] * frequency
    cosine = jnp.cos(angle)
    sine = jnp.sin(angle)
    first_half = values[..., :half_dim]
    second_half = values[..., half_dim:]
    return jnp.concatenate([first_half * cosine - second_half * sine, second_half * cosine + first_half * sine], axis=-1)

def reference(tokens, norm_gain, query_weight, query_bias, kv_weight, kv_bias, out_weight, shared_slot, shared_len, shared_owner, hist_pool, hist_pages, hist_len, req_len, req_offset, req_parent):
    features = tokens.astype(jnp.float32)
    mean_square = lax.optimization_barrier(jnp.mean(features * features, axis=1, keepdims=True))
    normed = (features * lax.rsqrt(mean_square + norm_eps) * norm_gain).astype(jnp.bfloat16)
    row_request, row_parent, position = request_layout(req_len, req_parent, hist_len, shared_len, TOK_DEV)
    flat_position = position.reshape(TOKENS)
    queries = jnp.dot(normed, query_weight, preferred_element_type=jnp.float32) + query_bias
    queries = rotate(queries.reshape(TOKENS, HEADS, HEAD_DIM), flat_position).astype(jnp.bfloat16)
    kv_rows = (jnp.dot(normed, kv_weight, preferred_element_type=jnp.float32) + kv_bias).reshape(TOKENS, KV_HEADS, 2, HEAD_DIM)
    new_keys = rotate(kv_rows[:, :, 0, :], flat_position)
    new_cache = jnp.stack([new_keys, kv_rows[:, :, 1, :]], axis=2).astype(jnp.bfloat16)
    slot_rows = shared_slot.reshape(SEQ_DEVS, SHARED_LEN, KV_HEADS, 2, HEAD_DIM)
    hot_rows = slot_rows[shared_owner].reshape((NODES1 + 1) * SHARED_LEN, KV_HEADS, 2, HEAD_DIM)
    hot_node = jnp.repeat(jnp.arange(NODES1 + 1, dtype=jnp.int32), SHARED_LEN)
    hot_place = jnp.tile(jnp.arange(SHARED_LEN, dtype=jnp.int32), NODES1 + 1)
    hot_valid = hot_place < jnp.repeat(shared_len, SHARED_LEN)
    pool_rows = hist_pool.reshape(SEQ_DEVS, REQ_DEV * PAGES, PAGE, KV_HEADS, 2, HEAD_DIM)
    steps_table = jnp.array(neighbour_steps, dtype=jnp.int32)
    hist_request = jnp.repeat(jnp.arange(REQ_DEV, dtype=jnp.int32), HIST_CAP)
    hist_place = jnp.tile(jnp.arange(HIST_CAP, dtype=jnp.int32), REQ_DEV)
    group_size = HEADS // KV_HEADS
    score_scale = HEAD_DIM ** (-0.5)
    row_index = jnp.arange(TOK_DEV, dtype=jnp.int32)

    def one_device(device):
        request_of = row_request[device]
        parent_of = row_parent[device]
        slot_of = req_offset[device]
        owner_of = (device + steps_table[slot_of]) % SEQ_DEVS
        page_ids = hist_pages[owner_of[:, None], slot_of[:, None] * PAGES + jnp.arange(PAGES, dtype=jnp.int32)[None, :]]
        history = pool_rows[owner_of[:, None], page_ids].reshape(REQ_DEV * HIST_CAP, KV_HEADS, 2, HEAD_DIM)
        fresh = lax.dynamic_slice_in_dim(new_cache, (device * TOK_DEV).astype(jnp.int32), TOK_DEV, 0)
        row_queries = lax.dynamic_slice_in_dim(queries, (device * TOK_DEV).astype(jnp.int32), TOK_DEV, 0)
        every_key = jnp.concatenate([hot_rows, history, fresh], axis=0)
        hot_mask = ((hot_node[None, :] == 0) | (hot_node[None, :] == parent_of[:, None] + 1)) & hot_valid[None, :]
        hist_valid = hist_place < hist_len[device][hist_request]
        hist_mask = (hist_request[None, :] == request_of[:, None]) & hist_valid[None, :]
        own_mask = (request_of[None, :] == request_of[:, None]) & (row_index[None, :] <= row_index[:, None])
        key_mask = jnp.concatenate([hot_mask, hist_mask, own_mask], axis=1)
        outputs = []
        for kv_group in range(KV_HEADS):
            head_queries = row_queries[:, kv_group * group_size:(kv_group + 1) * group_size, :].astype(jnp.float32)
            key_vectors = every_key[:, kv_group, 0, :].astype(jnp.float32)
            value_vectors = every_key[:, kv_group, 1, :].astype(jnp.float32)
            scores = jnp.einsum('rhd,kd->rhk', head_queries, key_vectors, precision=lax.Precision.HIGHEST) * score_scale
            scores = jnp.where(key_mask[:, None, :], scores, masked_score)
            top_score = lax.optimization_barrier(jnp.max(scores, axis=2, keepdims=True))
            weights = jnp.where(key_mask[:, None, :], jnp.exp(scores - top_score), 0.0)
            weight_sum = lax.optimization_barrier(jnp.sum(weights, axis=2, keepdims=True))
            rounded = lax.optimization_barrier(weights.astype(jnp.bfloat16)).astype(jnp.float32)
            mixed = jnp.einsum('rhk,kd->rhd', rounded, value_vectors, precision=lax.Precision.HIGHEST) / weight_sum
            outputs.append(mixed)
        return jnp.concatenate(outputs, axis=1).astype(jnp.bfloat16).reshape(TOK_DEV, HEADS * HEAD_DIM)
    attention = lax.map(one_device, jnp.arange(SEQ_DEVS, dtype=jnp.int32)).reshape(TOKENS, HEADS * HEAD_DIM)
    group_cols = HEADS * HEAD_DIM // N_TP
    summed = jnp.zeros((TOKENS, D), jnp.float32)
    for group_number in range(N_TP):
        term = jnp.dot(attention[:, group_number * group_cols:(group_number + 1) * group_cols], out_weight[group_number * group_cols:(group_number + 1) * group_cols], preferred_element_type=jnp.float32)
        summed = summed + lax.optimization_barrier(term.astype(jnp.bfloat16)).astype(jnp.float32)
    hidden = (summed + features).astype(jnp.bfloat16)
    return (hidden, new_cache.reshape(TOKENS, KV_HEADS * 2 * HEAD_DIM))
```

```python
import math

import jax
import jax.numpy as jnp
from jax import lax
from jax.sharding import Mesh, PartitionSpec as P

norm_eps = 1e-06
rope_base = 1000000.0
neighbour_steps = (-2, -1, 1, 2)
masked_score = -1e30
seq_axes = ("z", "y", "core")


def from_partner(shard, axis, apart):
    return lax.ppermute(shard, axis, [(i, i ^ 1 << apart) for i in range(lax.axis_size(axis))])


def copies_exchanged(block, axis, count):
    copies = jnp.broadcast_to(block[None], (count,) + block.shape)
    return lax.all_to_all(copies, axis, 0, 0, tiled=True)


def gathered_nodes(head_columns, shared_owner):
    z_count = lax.axis_size("z")
    plane_count = lax.axis_size("y") * lax.axis_size("core")
    rows, columns = head_columns.shape
    chunk = rows // plane_count
    pieces = head_columns.reshape(plane_count, chunk, columns)
    arrived = lax.all_to_all(pieces, ("y", "core"), 0, 0, tiled=True)
    in_plane = shared_owner % plane_count
    plane = shared_owner // plane_count
    node_total = shared_owner.shape[0]
    chosen = jnp.stack(
        [lax.dynamic_index_in_dim(arrived, in_plane[n], 0, False) for n in range(node_total)]
    )
    planes = copies_exchanged(chosen, "z", z_count)
    kept = jnp.stack(
        [lax.dynamic_index_in_dim(planes[:, n], plane[n], 0, False) for n in range(node_total)]
    )
    spread = lax.all_gather(kept, ("y", "core"), axis=0, tiled=False)
    return spread.reshape(plane_count * node_total * chunk, columns), chunk


def passed_along(block, axis, distance):
    devices = range(math.prod(lax.axis_size(name) for name in axis))
    route = [((i - distance) % len(devices), i) for i in devices]
    return lax.ppermute(block, axis, route)


def request_layout(req_len, req_parent, hist_len, shared_len, row_count):
    request_end = jnp.cumsum(req_len, axis=1)
    request_start = request_end - req_len
    row_index = jnp.arange(row_count, dtype=jnp.int32)
    row_request = jnp.sum(
        (row_index[None, :, None] >= request_end[:, None, :]).astype(jnp.int32), axis=2
    )
    slot_numbers = jnp.arange(req_len.shape[1], dtype=jnp.int32)
    chosen = row_request[:, :, None] == slot_numbers[None, None, :]

    def lookup(table):
        return jnp.sum(jnp.where(chosen, table[:, None, :], 0), axis=2)

    row_offset = row_index[None, :] - lookup(request_start)
    row_parent = lookup(req_parent)
    node_numbers = jnp.arange(shared_len.shape[0] - 1, dtype=jnp.int32)
    parent_length = jnp.sum(
        jnp.where(row_parent[:, :, None] == node_numbers, shared_len[1:], 0), axis=2
    )
    position = shared_len[0] + parent_length + lookup(hist_len) + row_offset
    return (row_request, row_parent, position)


def rotate(values, position):
    half_dim = values.shape[-1] // 2
    frequency = rope_base ** (-2.0 * jnp.arange(half_dim, dtype=jnp.float32) / values.shape[-1])
    angle = position.astype(jnp.float32)[:, None, None] * frequency
    cosine = jnp.cos(angle)
    sine = jnp.sin(angle)
    first_half = values[..., :half_dim]
    second_half = values[..., half_dim:]
    return jnp.concatenate(
        [first_half * cosine - second_half * sine, second_half * cosine + first_half * sine],
        axis=-1,
    )


def partial_attention(queries, key_vectors, value_vectors, key_mask):
    score_scale = queries.shape[-1] ** (-0.5)
    scores = (
        jnp.einsum("rhd,kd->rhk", queries, key_vectors, preferred_element_type=jnp.float32)
        * score_scale
    )
    scores = jnp.where(key_mask[:, None, :], scores, masked_score)
    top_score = jnp.max(scores, axis=2)
    weights = jnp.where(key_mask[:, None, :], jnp.exp(scores - top_score[:, :, None]), 0.0)
    weight_sum = jnp.sum(weights, axis=2)
    mixed = jnp.einsum(
        "rhk,kd->rhd",
        weights.astype(jnp.bfloat16),
        value_vectors,
        preferred_element_type=jnp.float32,
    )
    return (top_score, weight_sum, mixed)


def combine(first_part, second_part):
    top_score = jnp.maximum(first_part[0], second_part[0])
    first_scale = jnp.exp(first_part[0] - top_score)
    second_scale = jnp.exp(second_part[0] - top_score)
    weight_sum = first_part[1] * first_scale + second_part[1] * second_scale
    mixed = first_part[2] * first_scale[:, :, None] + second_part[2] * second_scale[:, :, None]
    return (top_score, weight_sum, mixed)


def on_device(
    tokens,
    norm_gain,
    query_weight,
    query_bias,
    kv_weight,
    kv_bias,
    out_weight,
    shared_slot,
    shared_len,
    shared_owner,
    hist_pool,
    hist_pages,
    hist_len,
    req_len,
    req_offset,
    req_parent,
):
    group_count = lax.axis_size("tp")
    features = jnp.concatenate(list(copies_exchanged(tokens, "tp", group_count)), axis=1)
    widened = features.astype(jnp.float32)
    mean_square = jnp.mean(widened * widened, axis=1, keepdims=True)
    normed = (widened * lax.rsqrt(mean_square + norm_eps) * norm_gain).astype(jnp.bfloat16)
    head_dim = kv_bias.shape[0]
    head_count = query_weight.shape[1] // head_dim
    row_count = features.shape[0]
    tp_index = lax.axis_index("tp")
    kv_group = tp_index // 2
    holds_key = tp_index % 2 == 0
    row_request, row_parent, position = request_layout(
        req_len, req_parent, hist_len, shared_len, row_count
    )
    row_request = row_request[0]
    row_parent = row_parent[0]
    position = position[0]
    queries = jnp.dot(normed, query_weight, preferred_element_type=jnp.float32) + query_bias
    queries = rotate(queries.reshape(row_count, head_count, head_dim), position).astype(
        jnp.bfloat16
    )
    own_block = jnp.dot(normed, kv_weight, preferred_element_type=jnp.float32) + kv_bias
    own_block = jnp.where(
        holds_key, rotate(own_block[:, None, :], position)[:, 0, :], own_block
    ).astype(jnp.bfloat16)
    partner = from_partner(own_block, "tp", 0)
    fresh_keys = jnp.where(holds_key, own_block, partner)
    fresh_values = jnp.where(holds_key, partner, own_block)
    head_columns = lax.dynamic_slice_in_dim(shared_slot, kv_group * 2 * head_dim, 2 * head_dim, 1)
    node_total = shared_owner.shape[0]
    hot_rows, chunk = gathered_nodes(head_columns, shared_owner)
    hot_index = jnp.arange(hot_rows.shape[0], dtype=jnp.int32)
    hot_node = hot_index // chunk % node_total
    hot_place = hot_index // (chunk * node_total) * chunk + hot_index % chunk
    hot_valid = hot_place < shared_len[hot_node]
    every_key = jnp.concatenate([hot_rows[:, :head_dim], fresh_keys], axis=0)
    every_value = jnp.concatenate([hot_rows[:, head_dim:], fresh_values], axis=0)
    block_rows = min(512, row_count)
    row_index = jnp.arange(row_count, dtype=jnp.int32)

    def local_block(block_number):
        row_start = block_number * block_rows
        block_places = row_start + jnp.arange(block_rows, dtype=jnp.int32)
        hot_mask = (
            (hot_node[None, :] == 0) | (hot_node[None, :] == row_parent[:, None] + 1)
        ) & hot_valid[None, :]
        own_mask = (row_request[None, :] == row_request[:, None]) & (
            row_index[None, :] <= block_places[:, None]
        )
        return partial_attention(
            queries, every_key, every_value, jnp.concatenate([hot_mask, own_mask], axis=1)
        )

    local_parts = lax.map(local_block, jnp.arange(row_count // block_rows, dtype=jnp.int32))
    local_parts = tuple((piece.reshape((row_count,) + piece.shape[2:]) for piece in local_parts))
    capacity = row_count // 2
    request_count = req_len.shape[1]
    page_count = hist_pages.shape[1] // request_count
    request_end = jnp.cumsum(req_len[0])
    request_start = request_end - req_len[0]
    padded_queries = jnp.concatenate(
        [queries, jnp.zeros((capacity, head_count, head_dim), jnp.bfloat16)], axis=0
    )
    history_top = jnp.full((row_count + capacity, head_count), masked_score, jnp.float32)
    history_sum = jnp.zeros((row_count + capacity, head_count), jnp.float32)
    history_mix = jnp.zeros((row_count + capacity, head_count, head_dim), jnp.float32)
    capacity_rows = jnp.arange(capacity, dtype=jnp.int32)
    for slot_number in range(request_count):
        offset_step = neighbour_steps[slot_number]
        chosen = req_offset[0] == slot_number
        row_start = jnp.sum(jnp.where(chosen, request_start, 0))
        row_total = jnp.sum(jnp.where(chosen, req_len[0], 0))
        node_depth = jnp.sum(jnp.where(chosen, hist_len[0], 0)).reshape(1)
        window = lax.dynamic_slice_in_dim(padded_queries, row_start, capacity, 0)
        page_rows = hist_pool[
            hist_pages[0, slot_number * page_count : (slot_number + 1) * page_count]
        ]
        flat_pages = page_rows.reshape(-1, page_rows.shape[-1])
        node_places = jnp.arange(flat_pages.shape[0], dtype=jnp.int32)
        node_rows = lax.dynamic_slice_in_dim(flat_pages, kv_group * 2 * head_dim, 2 * head_dim, 1)
        arrived_node = passed_along(node_rows, seq_axes, -offset_step)
        depth_mask = jnp.broadcast_to(
            (node_places < node_depth[0])[None, :], (capacity, flat_pages.shape[0])
        )
        answer = partial_attention(
            window, arrived_node[:, :head_dim], arrived_node[:, head_dim:], depth_mask
        )
        row_valid = capacity_rows < row_total

        def put_rows(whole_rows, fresh_part):
            region = lax.dynamic_slice_in_dim(whole_rows, row_start, capacity, 0)
            keep_rows = row_valid.reshape((capacity,) + (1,) * (fresh_part.ndim - 1))
            return lax.dynamic_update_slice_in_dim(
                whole_rows, jnp.where(keep_rows, fresh_part, region), row_start, 0
            )

        history_top = put_rows(history_top, answer[0])
        history_sum = put_rows(history_sum, answer[1])
        history_mix = put_rows(history_mix, answer[2])
    history_part = (history_top[:row_count], history_sum[:row_count], history_mix[:row_count])
    merged = combine(local_parts, history_part)
    attention = (
        (merged[2] / merged[1][:, :, None])
        .astype(jnp.bfloat16)
        .reshape(row_count, head_count * head_dim)
    )
    terms = jnp.dot(attention, out_weight, preferred_element_type=jnp.float32)
    width = tokens.shape[1]
    blocks = jnp.stack(
        [terms[:, g * width : (g + 1) * width].astype(jnp.bfloat16) for g in range(group_count)]
    )
    summed = jnp.sum(lax.all_to_all(blocks, "tp", 0, 0, tiled=True).astype(jnp.float32), axis=0)
    hidden = (summed + tokens.astype(jnp.float32)).astype(jnp.bfloat16)
    return (hidden, own_block)


def solution(mesh):
    devices = mesh.devices
    split = Mesh(devices.reshape(8, devices.shape[0] // 16, 2, devices.shape[1]), seq_axes + ("tp",))
    return jax.shard_map(
        on_device,
        mesh=split,
        in_specs=(
            P(seq_axes, "tp"),
            P(),
            P(None, "tp"),
            P("tp"),
            P(None, "tp"),
            P("tp"),
            P("tp", None),
            P(seq_axes, None),
            P(),
            P(),
            P(seq_axes, None, None),
            P(seq_axes, None),
            P(seq_axes, None),
            P(seq_axes, None),
            P(seq_axes, None),
            P(seq_axes, None),
        ),
        out_specs=(P(seq_axes, "tp"), P(seq_axes, "tp")),
        check_vma=False,
    )
```

```python
import math

import jax
import jax.numpy as jnp
from jax import lax
from jax.experimental import pallas as pl
from jax.experimental.pallas import tpu as pltpu
from jax.sharding import Mesh, PartitionSpec as P

norm_eps = 1e-06
rope_base = 1000000.0
neighbour_steps = (-2, -1, 1, 2)
seq_axes = ("z", "y", "core")
barred = -(2.0**100)
f32 = jnp.float32
bf16 = jnp.bfloat16
int32 = jnp.int32


def passed_along(block, axis, distance):
    devices = range(math.prod(lax.axis_size(name) for name in axis))
    return lax.ppermute(block, axis, [((i - distance) % len(devices), i) for i in devices])


def copies_exchanged(block, axis, count):
    copies = jnp.broadcast_to(block[None], (count,) + block.shape)
    return lax.all_to_all(copies, axis, 0, 0, tiled=True)


def gathered_nodes(head_columns, shared_owner):
    z_count = lax.axis_size("z")
    plane_count = lax.axis_size("y") * lax.axis_size("core")
    rows, columns = head_columns.shape
    chunk = rows // plane_count
    pieces = head_columns.reshape(plane_count, chunk, columns)
    arrived = lax.all_to_all(pieces, ("y", "core"), 0, 0, tiled=True)
    in_plane = shared_owner % plane_count
    plane = shared_owner // plane_count
    node_total = shared_owner.shape[0]
    chosen = jnp.stack(
        [lax.dynamic_index_in_dim(arrived, in_plane[n], 0, False) for n in range(node_total)]
    )
    planes = copies_exchanged(chosen, "z", z_count)
    kept = jnp.stack(
        [lax.dynamic_index_in_dim(planes[:, n], plane[n], 0, False) for n in range(node_total)]
    )
    return lax.all_gather(kept, ("y", "core"), axis=0, tiled=False)


def pages_kernel(page_ref, group_ref, pool_ref, *rest):
    outs, sems = rest[:-1], rest[-1]
    page_rows = pool_ref.shape[1]
    width = outs[0].shape[1]
    per_slot = outs[0].shape[0] // page_rows
    first = pl.multiple_of(group_ref[0] * width, width)
    copies = []
    for slot, out in enumerate(outs):
        for c in range(per_slot):
            n = slot * per_slot + c
            copies.append(
                pltpu.make_async_copy(
                    pool_ref.at[page_ref[n], :, pl.ds(first, width)],
                    out.at[pl.ds(c * page_rows, page_rows), :],
                    sems.at[n],
                )
            )
    for copy in copies:
        copy.start()
    for copy in copies:
        copy.wait()


def history_slots(hist_pool, pages, kv_group, slots, width):
    rows = pages.shape[0] // slots * hist_pool.shape[1]
    anywhere = pl.BlockSpec(memory_space=pl.ANY)
    return pl.pallas_call(
        pages_kernel,
        out_shape=[jax.ShapeDtypeStruct((rows, width), bf16)] * slots,
        grid_spec=pltpu.PrefetchScalarGridSpec(
            num_scalar_prefetch=2,
            grid=(),
            in_specs=[anywhere],
            out_specs=[anywhere] * slots,
            scratch_shapes=[pltpu.SemaphoreType.DMA((pages.shape[0],))],
        ),
        name="pages",
    )(pages, kv_group.reshape(1), hist_pool)


def projection_kernel(
    holds_ref, tok_ref, gain_ref, wq_ref, wkv_ref, qb_ref, kb_ref, cos_ref, sin_ref, q_ref, own_ref
):
    groups, rows, width = tok_ref.shape
    total = jnp.zeros((rows, 1), f32)
    for g in range(groups):
        block = tok_ref[g].astype(f32)
        total = total + jnp.sum(block * block, axis=1, keepdims=True)
    inverse = lax.rsqrt(total / (groups * width) + norm_eps)
    query = jnp.zeros((rows, wq_ref.shape[1]), f32)
    fresh = jnp.zeros((rows, wkv_ref.shape[1]), f32)
    for g in range(groups):
        span = pl.ds(g * width, width)
        normed = (tok_ref[g].astype(f32) * inverse * gain_ref[:, span]).astype(bf16)
        query = query + jnp.dot(normed, wq_ref[span, :], preferred_element_type=f32)
        fresh = fresh + jnp.dot(normed, wkv_ref[span, :], preferred_element_type=f32)
    cosine = cos_ref[...]
    sine = sin_ref[...]
    half = cosine.shape[1] // 2

    def turned(part):
        return part * cosine + pltpu.roll(part, half, 1) * sine

    query = query + qb_ref[...]
    dim = cosine.shape[1]
    for h in range(q_ref.shape[0]):
        q_ref[h] = turned(query[:, h * dim : (h + 1) * dim]).astype(bf16)
    fresh = fresh + kb_ref[...]

    @pl.when(holds_ref[0] == 1)
    def _():
        own_ref[...] = turned(fresh).astype(bf16)

    @pl.when(holds_ref[0] == 0)
    def _():
        own_ref[...] = fresh.astype(bf16)


def attention_kernel(
    info_ref, q_ref, own_ref, partner_ref, h0_ref, h1_ref, h2_ref, h3_ref, hot_ref, wo_ref,
    out_ref, key_ref, value_ref,
):
    heads, rows, dim = q_ref.shape
    hist_refs = (h0_ref, h1_ref, h2_ref, h3_ref)
    requests = len(hist_refs)
    starts = [info_ref[r] for r in range(requests)]
    hist_len = [info_ref[4 + r] for r in range(requests)]
    slot = [info_ref[8 + r] for r in range(requests)]
    parent = [info_ref[12 + r] for r in range(requests)]
    shared_len = [info_ref[16 + n] for n in range(5)]
    holds = info_ref[21]

    @pl.when(holds == 1)
    def _():
        key_ref[...] = own_ref[...]
        value_ref[...] = partner_ref[...]

    @pl.when(holds == 0)
    def _():
        key_ref[...] = partner_ref[...]
        value_ref[...] = own_ref[...]

    def by_request(index, values):
        picked = jnp.full(index.shape, values[0], int32)
        for r in range(1, requests):
            picked = jnp.where(index >= starts[r], values[r], picked)
        return picked

    row = lax.broadcasted_iota(int32, (rows, dim), 0)
    lane = lax.broadcasted_iota(int32, (rows, dim), 1)
    hit = (
        (lane == by_request(row, slot))
        | (lane == requests + by_request(row, parent))
        | (lane == 2 * requests)
    )
    marks = jnp.where(hit, 1.0, 0.0).astype(bf16)

    def bars(bad):
        return jnp.where(bad, barred, 0.0).astype(bf16)

    keys = []
    values = []
    for j in range(requests):
        deep = jnp.int32(0)
        for r in range(requests):
            deep = deep + jnp.where(slot[r] == j, hist_len[r], 0)
        place = lax.broadcasted_iota(int32, (hist_refs[j].shape[0], dim), 0)
        side = lax.broadcasted_iota(int32, (hist_refs[j].shape[0], dim), 1)
        bad = ((side < requests) & (side != j)) | ((side == 2 * requests) & (place >= deep))
        keys.append(jnp.concatenate([hist_refs[j][:, :dim], bars(bad)], axis=1))
        values.append(hist_refs[j][:, dim:])

    chunks, nodes, chunk, _ = hot_ref.shape
    index = lax.broadcasted_iota(int32, (nodes * chunk, dim), 0)
    side = lax.broadcasted_iota(int32, (nodes * chunk, dim), 1)
    node = jnp.zeros(index.shape, int32)
    left = jnp.full(index.shape, shared_len[0], int32)
    for n in range(1, nodes):
        node = jnp.where(index >= n * chunk, n, node)
        left = jnp.where(index >= n * chunk, shared_len[n], left)
    left = left - (index - node * chunk)
    other = (side >= requests) & (side < 2 * requests) & (node > 0) & (side != requests + node - 1)
    last = side == 2 * requests
    for s in range(chunks):
        block = hot_ref[s].reshape(nodes * chunk, 2 * dim)
        bad = other | (last & (left <= s * chunk))
        keys.append(jnp.concatenate([block[:, :dim], bars(bad)], axis=1))
        values.append(block[:, dim:])

    far_keys = jnp.concatenate(keys, axis=0)
    far_values = jnp.concatenate(values, axis=0)
    far_values = jnp.concatenate([far_values, jnp.ones_like(far_values)], axis=1)
    own_keys = key_ref[...]
    own_values = value_ref[...]
    own_values = jnp.concatenate([own_values, jnp.ones_like(own_values)], axis=1)

    wide_row = lax.broadcasted_iota(int32, (rows, rows), 0)
    wide_col = lax.broadcasted_iota(int32, (rows, rows), 1)
    numbers = list(range(requests))
    seen = (wide_col <= wide_row) & (by_request(wide_row, numbers) == by_request(wide_col, numbers))
    hidden_keys = jnp.where(seen, 0.0, barred)

    scale = dim ** (-0.5) * math.log2(math.e)
    across = (((1,), (1,)), ((), ()))
    merged = []
    for h in range(heads):
        query = q_ref[h]
        far = lax.dot_general(
            jnp.concatenate([query, marks], axis=1), far_keys, across, preferred_element_type=f32
        )
        own = lax.dot_general(query, own_keys, across, preferred_element_type=f32) + hidden_keys
        top = jnp.maximum(
            jnp.max(far, axis=1, keepdims=True), jnp.max(own, axis=1, keepdims=True)
        )
        far_weights = jnp.exp2((far - top) * scale).astype(bf16)
        own_weights = jnp.exp2((own - top) * scale).astype(bf16)
        mixed = jnp.dot(far_weights, far_values, preferred_element_type=f32) + jnp.dot(
            own_weights, own_values, preferred_element_type=f32
        )
        merged.append((mixed[:, :dim] / mixed[:, dim:]).astype(bf16))
    attention = jnp.concatenate(merged, axis=1)
    width = out_ref.shape[2]
    for g in range(out_ref.shape[0]):
        out_ref[g] = jnp.dot(
            attention, wo_ref[:, g * width : (g + 1) * width], preferred_element_type=f32
        ).astype(bf16)


def whole(count):
    return [pl.BlockSpec(memory_space=pltpu.VMEM)] * count


def on_device(
    tokens,
    norm_gain,
    query_weight,
    query_bias,
    kv_weight,
    kv_bias,
    out_weight,
    shared_slot,
    shared_len,
    shared_owner,
    hist_pool,
    hist_pages,
    hist_len,
    req_len,
    req_offset,
    req_parent,
):
    group_count = lax.axis_size("tp")
    row_count, width = tokens.shape
    head_dim = kv_bias.shape[0]
    head_count = query_weight.shape[1] // head_dim
    request_count = req_len.shape[1]
    tp_index = lax.axis_index("tp")
    kv_group = tp_index // 2
    holds_key = (tp_index % 2 == 0).astype(int32)
    scalars = pl.BlockSpec(memory_space=pltpu.SMEM)

    head_columns = lax.dynamic_slice_in_dim(shared_slot, kv_group * 2 * head_dim, 2 * head_dim, 1)
    hot = gathered_nodes(head_columns, shared_owner)
    features = copies_exchanged(tokens, "tp", group_count)
    slots = history_slots(hist_pool, hist_pages[0], kv_group, request_count, 2 * head_dim)
    histories = [
        passed_along(slots[j], seq_axes, -neighbour_steps[j]) for j in range(request_count)
    ]

    starts = jnp.cumsum(req_len[0]) - req_len[0]
    base = shared_len[0] + shared_len[1 + req_parent[0]] + hist_len[0] - starts
    row = jnp.arange(row_count, dtype=int32)[:, None]
    shift = jnp.broadcast_to(base[0], row.shape)
    for r in range(1, request_count):
        shift = jnp.where(row >= starts[r], base[r], shift)
    half = head_dim // 2
    frequency = rope_base ** (-2.0 * jnp.arange(half, dtype=f32) / head_dim)
    angle = (row + shift).astype(f32) * frequency[None, :]
    cosine = jnp.cos(angle)
    sine = jnp.sin(angle)
    cosine = jnp.concatenate([cosine, cosine], axis=1)
    sine = jnp.concatenate([-sine, sine], axis=1)

    queries, own_block = pl.pallas_call(
        projection_kernel,
        out_shape=[
            jax.ShapeDtypeStruct((head_count, row_count, head_dim), bf16),
            jax.ShapeDtypeStruct((row_count, head_dim), bf16),
        ],
        in_specs=[scalars] + whole(8),
        out_specs=whole(2),
        compiler_params=pltpu.CompilerParams(vmem_limit_bytes=32 * 2**20),
        name="projection",
    )(
        holds_key.reshape(1),
        features,
        norm_gain[None, :],
        query_weight,
        kv_weight,
        query_bias[None, :],
        kv_bias[None, :],
        cosine,
        sine,
    )
    partner = lax.ppermute(own_block, "tp", [(i, i ^ 1) for i in range(group_count)])
    info = jnp.concatenate(
        [starts, hist_len[0], req_offset[0], req_parent[0], shared_len, holds_key.reshape(1)]
    ).astype(int32)
    blocks = pl.pallas_call(
        attention_kernel,
        out_shape=jax.ShapeDtypeStruct((group_count, row_count, width), bf16),
        in_specs=[scalars] + whole(9),
        out_specs=whole(1)[0],
        scratch_shapes=[pltpu.VMEM((row_count, head_dim), bf16)] * 2,
        compiler_params=pltpu.CompilerParams(vmem_limit_bytes=48 * 2**20),
        name="attention",
    )(info, queries, own_block, partner, *histories, hot, out_weight)
    summed = jnp.sum(lax.all_to_all(blocks, "tp", 0, 0, tiled=True).astype(f32), axis=0)
    hidden = (summed + tokens.astype(f32)).astype(bf16)
    return (hidden, own_block)


def solution(mesh):
    devices = mesh.devices
    split = Mesh(devices.reshape(8, devices.shape[0] // 16, 2, devices.shape[1]), seq_axes + ("tp",))
    by_seq = P(seq_axes, None)
    return jax.shard_map(
        on_device,
        mesh=split,
        in_specs=(
            P(seq_axes, "tp"),
            P(),
            P(None, "tp"),
            P("tp"),
            P(None, "tp"),
            P("tp"),
            P("tp", None),
            by_seq,
            P(),
            P(),
            P(seq_axes, None, None),
            by_seq,
            by_seq,
            by_seq,
            by_seq,
            by_seq,
        ),
        out_specs=(P(seq_axes, "tp"), P(seq_axes, "tp")),
        check_vma=False,
    )
```

```python
import math

import jax
import jax.numpy as jnp
from jax import lax
from jax.experimental import pallas as pl
from jax.experimental.pallas import tpu as pltpu
from jax.sharding import Mesh, PartitionSpec as P

norm_eps = 1e-06
rope_base = 1000000.0
neighbour_steps = (-2, -1, 1, 2)
seq_axes = ("z", "y", "core")
barred = -(2.0**100)
f32 = jnp.float32
bf16 = jnp.bfloat16
int32 = jnp.int32


def passed_along(block, axis, distance):
    devices = range(math.prod(lax.axis_size(name) for name in axis))
    return lax.ppermute(block, axis, [((i - distance) % len(devices), i) for i in devices])


def scalars_from(info_ref, requests):
    names = ("length", "depth", "slot", "parent")
    table = {
        name: [info_ref[n * requests + r] for r in range(requests)] for n, name in enumerate(names)
    }
    starts = [jnp.int32(0)]
    for r in range(requests - 1):
        starts.append(starts[r] + table["length"][r])
    table["start"] = starts
    return table


def by_request(index, starts, values):
    picked = jnp.full(index.shape, values[0], int32)
    for r in range(1, len(starts)):
        picked = jnp.where(index >= starts[r], values[r], picked)
    return picked


def prepare_kernel(
    info_ref, page_ref, place_ref, pool_ref, pos_ref, *rest
):
    outs, sems = rest[:-1], rest[-1]
    page_rows = pool_ref.shape[1]
    width = outs[0].shape[1]
    per_slot = outs[0].shape[0] // page_rows
    first = pl.multiple_of(place_ref[0] // 2 * width, width)
    copies = []
    for slot, out in enumerate(outs):
        for c in range(per_slot):
            n = slot * per_slot + c
            copies.append(
                pltpu.make_async_copy(
                    pool_ref.at[page_ref[n], :, pl.ds(first, width)],
                    out.at[pl.ds(c * page_rows, page_rows), :],
                    sems.at[n],
                )
            )
    for copy in copies:
        copy.start()
    requests = len(outs)
    table = scalars_from(info_ref, requests)
    base = []
    for r in range(requests):
        above = info_ref[4 * requests + 1 + table["parent"][r]]
        base.append(info_ref[4 * requests] + above + table["depth"][r] - table["start"][r])
    row = lax.broadcasted_iota(int32, pos_ref.shape, 0)
    pos_ref[...] = (row + by_request(row, table["start"], base)).astype(f32)
    for copy in copies:
        copy.wait()


def prepared(info, pages, place, hist_pool, row_count, slots, width):
    rows = pages.shape[0] // slots * hist_pool.shape[1]
    scalars = pl.BlockSpec(memory_space=pltpu.SMEM)
    anywhere = pl.BlockSpec(memory_space=pl.ANY)
    return pl.pallas_call(
        prepare_kernel,
        out_shape=[jax.ShapeDtypeStruct((row_count, width // 2), f32)]
        + [jax.ShapeDtypeStruct((rows, width), bf16)] * slots,
        in_specs=[scalars] * 3 + [anywhere],
        out_specs=whole(1 + slots),
        scratch_shapes=[pltpu.SemaphoreType.DMA((pages.shape[0],))],
        name="prepare",
    )(info, pages, place, hist_pool)


def first_pick_kernel(owner_ref, arrived_ref, out_ref):
    per_plane = arrived_ref.shape[0]
    for n in range(out_ref.shape[1]):
        chosen = arrived_ref[lax.rem(owner_ref[n], per_plane)]
        for z in range(out_ref.shape[0]):
            out_ref[z, n] = chosen


def first_pick(owner, arrived, planes):
    return pl.pallas_call(
        first_pick_kernel,
        out_shape=jax.ShapeDtypeStruct((planes, owner.shape[0]) + arrived.shape[1:], bf16),
        in_specs=[pl.BlockSpec(memory_space=pltpu.SMEM)] + whole(1),
        out_specs=whole(1)[0],
        name="first_pick",
    )(owner, arrived)


def second_pick(owner, planes, per_plane, copies):
    def kernel(owner_ref, planes_ref, out_ref):
        for n in range(out_ref.shape[1]):
            chosen = planes_ref[lax.div(owner_ref[n], per_plane), n]
            for c in range(copies):
                out_ref[c, n] = chosen

    return pl.pallas_call(
        kernel,
        out_shape=jax.ShapeDtypeStruct((copies,) + planes.shape[1:], bf16),
        in_specs=[pl.BlockSpec(memory_space=pltpu.SMEM)] + whole(1),
        out_specs=whole(1)[0],
        name="second_pick",
    )(owner, planes)


def projection_kernel(
    place_ref, tok_ref, gain_ref, wq_ref, wkv_ref, qb_ref, kb_ref, cos_ref, sin_ref, q_ref, own_ref
):
    groups, rows, width = tok_ref.shape
    total = jnp.zeros((rows, 1), f32)
    for g in range(groups):
        block = tok_ref[g].astype(f32)
        total = total + jnp.sum(block * block, axis=1, keepdims=True)
    inverse = lax.rsqrt(total / (groups * width) + norm_eps)
    query = jnp.zeros((rows, wq_ref.shape[1]), f32)
    fresh = jnp.zeros((rows, wkv_ref.shape[1]), f32)
    for g in range(groups):
        span = pl.ds(g * width, width)
        normed = (tok_ref[g].astype(f32) * inverse * gain_ref[:, span]).astype(bf16)
        query = query + jnp.dot(normed, wq_ref[span, :], preferred_element_type=f32)
        fresh = fresh + jnp.dot(normed, wkv_ref[span, :], preferred_element_type=f32)
    cosine = cos_ref[...]
    sine = sin_ref[...]
    half = cosine.shape[1] // 2

    def turned(part):
        return part * cosine + pltpu.roll(part, half, 1) * sine

    query = query + qb_ref[...]
    dim = cosine.shape[1]
    for h in range(q_ref.shape[0]):
        q_ref[h] = turned(query[:, h * dim : (h + 1) * dim]).astype(bf16)
    fresh = fresh + kb_ref[...]

    @pl.when(place_ref[0] % 2 == 0)
    def _():
        own_ref[...] = turned(fresh).astype(bf16)

    @pl.when(place_ref[0] % 2 == 1)
    def _():
        own_ref[...] = fresh.astype(bf16)


def bars(bad):
    return jnp.where(bad, barred, 0.0).astype(bf16)


across = (((1,), (1,)), ((), ()))


def scale_of(dim):
    return dim ** (-0.5) * math.log2(math.e)


def local_kernel(
    info_ref, place_ref, q_ref, own_ref, partner_ref, h0_ref, h1_ref, h2_ref, h3_ref,
    mixed_ref, top_ref, marks_ref, bars_ref, key_ref, value_ref,
):
    heads, rows, dim = q_ref.shape
    hist_refs = (h0_ref, h1_ref, h2_ref, h3_ref)
    requests = len(hist_refs)
    table = scalars_from(info_ref, requests)
    starts, hist_len, slot, parent = (table[n] for n in ("start", "depth", "slot", "parent"))
    nodes = info_ref.shape[0] - 4 * requests
    shared_len = [info_ref[4 * requests + n] for n in range(nodes)]

    @pl.when(place_ref[0] % 2 == 0)
    def _():
        key_ref[...] = own_ref[...]
        value_ref[...] = partner_ref[...]

    @pl.when(place_ref[0] % 2 == 1)
    def _():
        key_ref[...] = partner_ref[...]
        value_ref[...] = own_ref[...]

    row = lax.broadcasted_iota(int32, (rows, dim), 0)
    lane = lax.broadcasted_iota(int32, (rows, dim), 1)
    hit = (
        (lane == by_request(row, starts, slot))
        | (lane == requests + by_request(row, starts, parent))
        | (lane == 2 * requests)
    )
    marks = jnp.where(hit, 1.0, 0.0).astype(bf16)
    marks_ref[...] = marks

    chunks, per_chunk, _ = bars_ref.shape
    chunk = per_chunk // nodes
    index = lax.broadcasted_iota(int32, (per_chunk, dim), 0)
    side = lax.broadcasted_iota(int32, (per_chunk, dim), 1)
    node = jnp.zeros(index.shape, int32)
    left = jnp.full(index.shape, shared_len[0], int32)
    for n in range(1, nodes):
        node = jnp.where(index >= n * chunk, n, node)
        left = jnp.where(index >= n * chunk, shared_len[n], left)
    left = left - (index - node * chunk)
    other = (side >= requests) & (side < 2 * requests) & (node > 0) & (side != requests + node - 1)
    last = side == 2 * requests
    for s in range(chunks):
        bars_ref[s] = bars(other | (last & (left <= s * chunk)))

    keys = []
    values = []
    for j in range(requests):
        deep = jnp.int32(0)
        for r in range(requests):
            deep = deep + jnp.where(slot[r] == j, hist_len[r], 0)
        place = lax.broadcasted_iota(int32, (hist_refs[j].shape[0], dim), 0)
        side = lax.broadcasted_iota(int32, (hist_refs[j].shape[0], dim), 1)
        bad = ((side < requests) & (side != j)) | ((side == 2 * requests) & (place >= deep))
        keys.append(jnp.concatenate([hist_refs[j][:, :dim], bars(bad)], axis=1))
        values.append(hist_refs[j][:, dim:])
    far_keys = jnp.concatenate(keys, axis=0)
    far_values = jnp.concatenate(values, axis=0)
    far_values = jnp.concatenate([far_values, jnp.ones_like(far_values)], axis=1)
    own_keys = key_ref[...]
    own_values = value_ref[...]
    own_values = jnp.concatenate([own_values, jnp.ones_like(own_values)], axis=1)

    wide_row = lax.broadcasted_iota(int32, (rows, rows), 0)
    wide_col = lax.broadcasted_iota(int32, (rows, rows), 1)
    numbers = list(range(requests))
    same = by_request(wide_row, starts, numbers) == by_request(wide_col, starts, numbers)
    unseen = jnp.where((wide_col <= wide_row) & same, 0.0, barred)

    scale = scale_of(dim)
    for h in range(heads):
        query = q_ref[h]
        far = lax.dot_general(
            jnp.concatenate([query, marks], axis=1), far_keys, across, preferred_element_type=f32
        )
        own = lax.dot_general(query, own_keys, across, preferred_element_type=f32) + unseen
        top = jnp.maximum(
            jnp.max(far, axis=1, keepdims=True), jnp.max(own, axis=1, keepdims=True)
        )
        far_weights = jnp.exp2((far - top) * scale).astype(bf16)
        own_weights = jnp.exp2((own - top) * scale).astype(bf16)
        mixed_ref[h] = jnp.dot(far_weights, far_values, preferred_element_type=f32) + jnp.dot(
            own_weights, own_values, preferred_element_type=f32
        )
        top_ref[h] = jnp.broadcast_to(top, (rows, dim))


def shared_kernel(q_ref, mixed_ref, top_ref, marks_ref, bars_ref, hot_ref, wo_ref, out_ref):
    heads, rows, dim = q_ref.shape
    chunks, nodes, chunk, _ = hot_ref.shape
    hot = hot_ref[...].reshape(chunks * nodes * chunk, 2 * dim)
    keys = jnp.concatenate([hot[:, :dim], bars_ref[...].reshape(-1, dim)], axis=1)
    values = hot[:, dim:]
    values = jnp.concatenate([values, jnp.ones_like(values)], axis=1)
    marks = marks_ref[...]
    scale = scale_of(dim)
    merged = []
    for h in range(heads):
        scores = lax.dot_general(
            jnp.concatenate([q_ref[h], marks], axis=1), keys, across, preferred_element_type=f32
        )
        top = jnp.maximum(jnp.max(scores, axis=1, keepdims=True), top_ref[h][:, :1])
        weights = jnp.exp2((scores - top) * scale).astype(bf16)
        kept = jnp.exp2((top_ref[h] - top) * scale)
        local = mixed_ref[h]
        mixed = jnp.dot(weights, values, preferred_element_type=f32)
        total = mixed[:, dim:] + local[:, dim:] * kept
        merged.append(((mixed[:, :dim] + local[:, :dim] * kept) / total).astype(bf16))
    attention = jnp.concatenate(merged, axis=1)
    width = out_ref.shape[2]
    for g in range(out_ref.shape[0]):
        out_ref[g] = jnp.dot(
            attention, wo_ref[:, g * width : (g + 1) * width], preferred_element_type=f32
        ).astype(bf16)


def whole(count):
    return [pl.BlockSpec(memory_space=pltpu.VMEM)] * count


def on_device(
    tokens,
    norm_gain,
    query_weight,
    query_bias,
    kv_weight,
    kv_bias,
    out_weight,
    shared_slot,
    shared_len,
    shared_owner,
    hist_pool,
    hist_pages,
    hist_len,
    req_len,
    req_offset,
    req_parent,
):
    group_count = lax.axis_size("tp")
    row_count, width = tokens.shape
    head_dim = kv_bias.shape[0]
    head_count = query_weight.shape[1] // head_dim
    request_count = req_len.shape[1]
    tp_index = lax.axis_index("tp")
    place = jnp.stack([tp_index, lax.axis_index("core")]).astype(int32)
    scalars = pl.BlockSpec(memory_space=pltpu.SMEM)

    copies = jnp.broadcast_to(tokens[None], (group_count,) + tokens.shape)
    features = lax.all_to_all(copies, "tp", 0, 0, tiled=True)
    info = jnp.concatenate([req_len[0], hist_len[0], req_offset[0], req_parent[0], shared_len])
    position, *slots = prepared(
        info, hist_pages[0], place, hist_pool, row_count, request_count, 2 * head_dim
    )
    z_count, y_count, core_count = (lax.axis_size(name) for name in seq_axes)
    plane_count = y_count * core_count
    chunk = shared_slot.shape[0] // plane_count
    node_total = shared_owner.shape[0]

    def history(j):
        return passed_along(slots[j], seq_axes, -neighbour_steps[j])

    def after(value, *others):
        return lax.optimization_barrier((value, *others))[0]

    histories = []
    pieces = lax.dynamic_slice_in_dim(shared_slot, tp_index // 2 * 2 * head_dim, 2 * head_dim, 1)
    pieces = after(pieces, features, slots[3])
    arrived = lax.all_to_all(
        pieces.reshape(plane_count, chunk, -1), seq_axes[1:], 0, 0, tiled=True
    )

    half = head_dim // 2
    frequency = rope_base ** (-2.0 * jnp.arange(half, dtype=f32) / head_dim)
    angle = position[:, :half] * frequency[None, :]
    cosine = jnp.cos(angle)
    sine = jnp.sin(angle)
    cosine = jnp.concatenate([cosine, cosine], axis=1)
    sine = jnp.concatenate([-sine, sine], axis=1)
    queries, own_block = pl.pallas_call(
        projection_kernel,
        out_shape=[
            jax.ShapeDtypeStruct((head_count, row_count, head_dim), bf16),
            jax.ShapeDtypeStruct((row_count, head_dim), bf16),
        ],
        in_specs=[scalars] + whole(8),
        out_specs=whole(2),
        compiler_params=pltpu.CompilerParams(vmem_limit_bytes=32 * 2**20),
        name="projection",
    )(
        place,
        features,
        norm_gain[None, :],
        query_weight,
        kv_weight,
        query_bias[None, :],
        kv_bias[None, :],
        cosine,
        sine,
    )
    partner = lax.ppermute(own_block, "tp", [(i, i ^ 1) for i in range(group_count)])
    slots[1] = after(slots[1], pieces)
    histories += [history(0), history(1)]
    chosen = first_pick(shared_owner, after(arrived, own_block, *histories), z_count)
    planes = lax.all_to_all(chosen, "z", 0, 0, tiled=True)
    slots[2] = after(slots[2], chosen)
    slots[3] = after(slots[3], chosen)
    histories += [history(2), history(3)]
    local = pl.pallas_call(
        local_kernel,
        out_shape=[
            jax.ShapeDtypeStruct((head_count, row_count, 2 * head_dim), f32),
            jax.ShapeDtypeStruct((head_count, row_count, head_dim), f32),
            jax.ShapeDtypeStruct((row_count, head_dim), bf16),
            jax.ShapeDtypeStruct((plane_count, node_total * chunk, head_dim), bf16),
        ],
        in_specs=[scalars] * 2 + whole(7),
        out_specs=whole(4),
        scratch_shapes=[pltpu.VMEM((row_count, head_dim), bf16)] * 2,
        compiler_params=pltpu.CompilerParams(vmem_limit_bytes=40 * 2**20),
        name="local",
    )(info, place, queries, own_block, partner, *histories)
    kept = second_pick(shared_owner, after(planes, *local), plane_count, 1)[0]
    hot = lax.all_gather(kept, seq_axes[1:], axis=0, tiled=False)
    blocks = pl.pallas_call(
        shared_kernel,
        out_shape=jax.ShapeDtypeStruct((group_count, row_count, width), bf16),
        in_specs=whole(7),
        out_specs=whole(1)[0],
        compiler_params=pltpu.CompilerParams(vmem_limit_bytes=40 * 2**20),
        name="shared",
    )(queries, *local, hot, out_weight)
    summed = jnp.sum(lax.all_to_all(blocks, "tp", 0, 0, tiled=True).astype(f32), axis=0)
    hidden = (summed + tokens.astype(f32)).astype(bf16)
    return (hidden, own_block)


def solution(mesh):
    devices = mesh.devices
    split = Mesh(devices.reshape(8, devices.shape[0] // 16, 2, devices.shape[1]), seq_axes + ("tp",))
    by_seq = P(seq_axes, None)
    return jax.shard_map(
        on_device,
        mesh=split,
        in_specs=(
            P(seq_axes, "tp"),
            P(),
            P(None, "tp"),
            P("tp"),
            P(None, "tp"),
            P("tp"),
            P("tp", None),
            by_seq,
            P(),
            P(),
            P(seq_axes, None, None),
            by_seq,
            by_seq,
            by_seq,
            by_seq,
            by_seq,
        ),
        out_specs=(P(seq_axes, "tp"), P(seq_axes, "tp")),
        check_vma=False,
    )
```

```python
import functools
import math

import jax
import jax.numpy as jnp
from jax import lax
from jax.experimental import pallas as pl
from jax.experimental.pallas import tpu as pltpu
from jax.sharding import Mesh, PartitionSpec as P

norm_eps = 1e-06
rope_base = 1000000.0
neighbour_steps = (-2, -1, 1, 2)
seq_axes = ("z", "y", "core")
barred = -(2.0**100)
f32 = jnp.float32
bf16 = jnp.bfloat16
int32 = jnp.int32


def passed_along(block, axis, distance):
    devices = range(math.prod(lax.axis_size(name) for name in axis))
    return lax.ppermute(block, axis, [((i - distance) % len(devices), i) for i in devices])


def scalars_from(info_ref, requests):
    names = ("length", "depth", "slot", "parent")
    table = {
        name: [info_ref[n * requests + r] for r in range(requests)] for n, name in enumerate(names)
    }
    starts = [jnp.int32(0)]
    for r in range(requests - 1):
        starts.append(starts[r] + table["length"][r])
    table["start"] = starts
    return table


def by_request(index, starts, values):
    picked = jnp.full(index.shape, values[0], int32)
    for r in range(1, len(starts)):
        picked = jnp.where(index >= starts[r], values[r], picked)
    return picked


def prepare_kernel(
    info_ref, page_ref, place_ref, pool_ref, pos_ref, *rest
):
    outs, sems = rest[:-1], rest[-1]
    page_rows = pool_ref.shape[1]
    width = outs[0].shape[1]
    per_slot = outs[0].shape[0] // page_rows
    first = pl.multiple_of(place_ref[0] // 2 * width, width)
    copies = []
    for slot, out in enumerate(outs):
        for c in range(per_slot):
            n = slot * per_slot + c
            copies.append(
                pltpu.make_async_copy(
                    pool_ref.at[page_ref[n], :, pl.ds(first, width)],
                    out.at[pl.ds(c * page_rows, page_rows), :],
                    sems.at[n],
                )
            )
    for copy in copies:
        copy.start()
    requests = len(outs)
    table = scalars_from(info_ref, requests)
    base = []
    for r in range(requests):
        above = info_ref[4 * requests + 1 + table["parent"][r]]
        base.append(info_ref[4 * requests] + above + table["depth"][r] - table["start"][r])
    row = lax.broadcasted_iota(int32, pos_ref.shape, 0)
    pos_ref[...] = (row + by_request(row, table["start"], base)).astype(f32)
    for copy in copies:
        copy.wait()


def prepared(info, pages, place, hist_pool, row_count, slots, width):
    rows = pages.shape[0] // slots * hist_pool.shape[1]
    scalars = pl.BlockSpec(memory_space=pltpu.SMEM)
    anywhere = pl.BlockSpec(memory_space=pl.ANY)
    return pl.pallas_call(
        prepare_kernel,
        out_shape=[jax.ShapeDtypeStruct((row_count, width // 2), f32)]
        + [jax.ShapeDtypeStruct((rows, width), bf16)] * slots,
        in_specs=[scalars] * 3 + [anywhere],
        out_specs=whole(1 + slots),
        scratch_shapes=[pltpu.SemaphoreType.DMA((pages.shape[0],))],
        compiler_params=pltpu.CompilerParams(vmem_limit_bytes=4 * 2**20),
        name="prepare",
    )(info, pages, place, hist_pool)


def first_pick_kernel(owner_ref, arrived_ref, out_ref):
    per_plane = arrived_ref.shape[0]
    for n in range(out_ref.shape[1]):
        chosen = arrived_ref[lax.rem(owner_ref[n], per_plane)]
        for z in range(out_ref.shape[0]):
            out_ref[z, n] = chosen


def first_pick(owner, arrived, planes):
    return pl.pallas_call(
        first_pick_kernel,
        out_shape=jax.ShapeDtypeStruct((planes, owner.shape[0]) + arrived.shape[1:], bf16),
        in_specs=[pl.BlockSpec(memory_space=pltpu.SMEM)] + whole(1),
        out_specs=whole(1)[0],
        compiler_params=pltpu.CompilerParams(vmem_limit_bytes=4 * 2**20),
        name="first_pick",
    )(owner, arrived)


def second_pick(owner, planes, per_plane, copies):
    def kernel(owner_ref, planes_ref, out_ref):
        for n in range(out_ref.shape[1]):
            chosen = planes_ref[lax.div(owner_ref[n], per_plane), n]
            for c in range(copies):
                out_ref[c, n] = chosen

    return pl.pallas_call(
        kernel,
        out_shape=jax.ShapeDtypeStruct((copies,) + planes.shape[1:], bf16),
        in_specs=[pl.BlockSpec(memory_space=pltpu.SMEM)] + whole(1),
        out_specs=whole(1)[0],
        name="second_pick",
    )(owner, planes)


def projection_kernel(
    place_ref, tok_ref, gain_ref, wq_ref, wkv_ref, qb_ref, kb_ref, cos_ref, sin_ref,
    q_ref, own_ref, kept_ref
):
    groups, rows, width = tok_ref.shape
    total = jnp.zeros((rows, 1), f32)
    for g in range(groups):
        block = tok_ref[g].astype(f32)
        total = total + jnp.sum(block * block, axis=1, keepdims=True)
    inverse = lax.rsqrt(total / (groups * width) + norm_eps)
    query = jnp.zeros((rows, wq_ref.shape[1]), f32)
    fresh = jnp.zeros((rows, wkv_ref.shape[1]), f32)
    for g in range(groups):
        span = pl.ds(g * width, width)
        normed = (tok_ref[g].astype(f32) * inverse * gain_ref[:, span]).astype(bf16)
        query = query + jnp.dot(normed, wq_ref[span, :], preferred_element_type=f32)
        fresh = fresh + jnp.dot(normed, wkv_ref[span, :], preferred_element_type=f32)
    cosine = cos_ref[...]
    sine = sin_ref[...]
    half = cosine.shape[1] // 2

    def turned(part):
        return part * cosine + pltpu.roll(part, half, 1) * sine

    query = query + qb_ref[...]
    dim = cosine.shape[1]
    for h in range(q_ref.shape[0]):
        q_ref[h] = turned(query[:, h * dim : (h + 1) * dim]).astype(bf16)
    fresh = fresh + kb_ref[...]

    @pl.when(place_ref[0] % 2 == 0)
    def _():
        own_ref[...] = turned(fresh).astype(bf16)
        kept_ref[...] = turned(fresh).astype(bf16)

    @pl.when(place_ref[0] % 2 == 1)
    def _():
        own_ref[...] = fresh.astype(bf16)
        kept_ref[...] = fresh.astype(bf16)


def bars(bad):
    return jnp.where(bad, barred, 0.0).astype(bf16)


across = (((1,), (1,)), ((), ()))


def scale_of(dim):
    return dim ** (-0.5) * math.log2(math.e)


def local_kernel(
    chunk, info_ref, place_ref, q_ref, own_ref, partner_ref, h0_ref, h1_ref, h2_ref, h3_ref,
    mixed_ref, top_ref, bars_ref, key_ref, value_ref,
):
    heads, rows, dim = q_ref.shape
    hist_refs = (h0_ref, h1_ref, h2_ref, h3_ref)
    requests = len(hist_refs)
    table = scalars_from(info_ref, requests)
    starts, hist_len, slot, parent = (table[n] for n in ("start", "depth", "slot", "parent"))
    nodes = info_ref.shape[0] - 4 * requests
    shared_len = [info_ref[4 * requests + n] for n in range(nodes)]

    @pl.when(place_ref[0] % 2 == 0)
    def _():
        key_ref[...] = own_ref[...]
        value_ref[...] = partner_ref[...]

    @pl.when(place_ref[0] % 2 == 1)
    def _():
        key_ref[...] = partner_ref[...]
        value_ref[...] = own_ref[...]

    row = lax.broadcasted_iota(int32, (rows, dim), 0)
    lane = lax.broadcasted_iota(int32, (rows, dim), 1)
    hit = (
        (lane == by_request(row, starts, slot))
        | (lane == requests + by_request(row, starts, parent))
        | (lane == 2 * requests)
    )
    marks = jnp.where(hit, 1.0, 0.0).astype(bf16)
    shared_rows = bars_ref.shape[0] - rows
    bars_ref[shared_rows:, :] = marks

    per_chunk = chunk * nodes
    chunks = shared_rows // per_chunk
    index = lax.broadcasted_iota(int32, (per_chunk, dim), 0)
    side = lax.broadcasted_iota(int32, (per_chunk, dim), 1)
    node = jnp.zeros(index.shape, int32)
    left = jnp.full(index.shape, shared_len[0], int32)
    for n in range(1, nodes):
        node = jnp.where(index >= n * chunk, n, node)
        left = jnp.where(index >= n * chunk, shared_len[n], left)
    left = left - (index - node * chunk)
    other = (side >= requests) & (side < 2 * requests) & (node > 0) & (side != requests + node - 1)
    last = side == 2 * requests
    for s in range(chunks):
        bars_ref[s * per_chunk : (s + 1) * per_chunk, :] = bars(other | (last & (left <= s * chunk)))

    keys = []
    values = []
    for j in range(requests):
        deep = jnp.int32(0)
        for r in range(requests):
            deep = deep + jnp.where(slot[r] == j, hist_len[r], 0)
        place = lax.broadcasted_iota(int32, (hist_refs[j].shape[0], dim), 0)
        side = lax.broadcasted_iota(int32, (hist_refs[j].shape[0], dim), 1)
        bad = ((side < requests) & (side != j)) | ((side == 2 * requests) & (place >= deep))
        keys.append(jnp.concatenate([hist_refs[j][:, :dim], bars(bad)], axis=1))
        values.append(hist_refs[j][:, dim:])
    far_keys = jnp.concatenate(keys, axis=0)
    far_values = jnp.concatenate(values, axis=0)
    far_values = jnp.concatenate([far_values, jnp.ones_like(far_values)], axis=1)
    own_keys = key_ref[...]
    own_values = value_ref[...]
    own_values = jnp.concatenate([own_values, jnp.ones_like(own_values)], axis=1)

    wide_row = lax.broadcasted_iota(int32, (rows, rows), 0)
    wide_col = lax.broadcasted_iota(int32, (rows, rows), 1)
    numbers = list(range(requests))
    same = by_request(wide_row, starts, numbers) == by_request(wide_col, starts, numbers)
    unseen = jnp.where((wide_col <= wide_row) & same, 0.0, barred)

    scale = scale_of(dim)
    for h in range(heads):
        query = q_ref[h]
        far = lax.dot_general(
            jnp.concatenate([query, marks], axis=1), far_keys, across, preferred_element_type=f32
        )
        own = lax.dot_general(query, own_keys, across, preferred_element_type=f32) + unseen
        top = jnp.maximum(
            jnp.max(far, axis=1, keepdims=True), jnp.max(own, axis=1, keepdims=True)
        )
        far_weights = jnp.exp2((far - top) * scale).astype(bf16)
        own_weights = jnp.exp2((own - top) * scale).astype(bf16)
        mixed_ref[h] = jnp.dot(far_weights, far_values, preferred_element_type=f32) + jnp.dot(
            own_weights, own_values, preferred_element_type=f32
        )
        top_ref[h] = jnp.broadcast_to(top, (rows, dim))


def shared_kernel(q_ref, mixed_ref, top_ref, bars_ref, hot_ref, wo_ref, out_ref):
    heads, rows, dim = q_ref.shape
    chunks, nodes, chunk, _ = hot_ref.shape
    hot = hot_ref[...].reshape(chunks * nodes * chunk, 2 * dim)
    keys = jnp.concatenate([hot[:, :dim], bars_ref[: hot.shape[0], :]], axis=1)
    values = hot[:, dim:]
    values = jnp.concatenate([values, jnp.ones_like(values)], axis=1)
    marks = bars_ref[hot.shape[0] :, :]
    scale = scale_of(dim)
    merged = []
    for h in range(heads):
        scores = lax.dot_general(
            jnp.concatenate([q_ref[h], marks], axis=1), keys, across, preferred_element_type=f32
        )
        top = jnp.maximum(jnp.max(scores, axis=1, keepdims=True), top_ref[h][:, :1])
        weights = jnp.exp2((scores - top) * scale).astype(bf16)
        kept = jnp.exp2((top_ref[h] - top) * scale)
        local = mixed_ref[h]
        mixed = jnp.dot(weights, values, preferred_element_type=f32)
        total = mixed[:, dim:] + local[:, dim:] * kept
        merged.append(((mixed[:, :dim] + local[:, :dim] * kept) / total).astype(bf16))
    attention = jnp.concatenate(merged, axis=1)
    width = out_ref.shape[2]
    for g in range(out_ref.shape[0]):
        out_ref[g] = jnp.dot(
            attention, wo_ref[:, g * width : (g + 1) * width], preferred_element_type=f32
        ).astype(bf16)


def whole(count):
    return [pl.BlockSpec(memory_space=pltpu.VMEM)] * count


def on_device(
    tokens,
    norm_gain,
    query_weight,
    query_bias,
    kv_weight,
    kv_bias,
    out_weight,
    shared_slot,
    shared_len,
    shared_owner,
    hist_pool,
    hist_pages,
    hist_len,
    req_len,
    req_offset,
    req_parent,
):
    group_count = lax.axis_size("tp")
    row_count, width = tokens.shape
    head_dim = kv_bias.shape[0]
    head_count = query_weight.shape[1] // head_dim
    request_count = req_len.shape[1]
    tp_index = lax.axis_index("tp")
    place = jnp.stack([tp_index, lax.axis_index("core")]).astype(int32)
    scalars = pl.BlockSpec(memory_space=pltpu.SMEM)

    copies = jnp.broadcast_to(tokens[None], (group_count,) + tokens.shape)
    features = lax.all_to_all(copies, "tp", 0, 0, tiled=True)
    info = jnp.concatenate([req_len[0], hist_len[0], req_offset[0], req_parent[0], shared_len])
    position, *slots = prepared(
        info, hist_pages[0], place, hist_pool, row_count, request_count, 2 * head_dim
    )
    z_count, y_count, core_count = (lax.axis_size(name) for name in seq_axes)
    plane_count = y_count * core_count
    chunk = shared_slot.shape[0] // plane_count
    node_total = shared_owner.shape[0]

    def history(j):
        return passed_along(slots[j], seq_axes, -neighbour_steps[j])

    def after(value, *others):
        return lax.optimization_barrier((value, *others))[0]

    histories = []
    pieces = lax.dynamic_slice_in_dim(shared_slot, tp_index // 2 * 2 * head_dim, 2 * head_dim, 1)
    pieces = after(pieces, features, slots[3])
    arrived = lax.all_to_all(
        pieces.reshape(plane_count, chunk, -1), seq_axes[1:], 0, 0, tiled=True
    )

    half = head_dim // 2
    frequency = rope_base ** (-2.0 * jnp.arange(half, dtype=f32) / head_dim)
    angle = position[:, :half] * frequency[None, :]
    cosine = jnp.cos(angle)
    sine = jnp.sin(angle)
    cosine = jnp.concatenate([cosine, cosine], axis=1)
    sine = jnp.concatenate([-sine, sine], axis=1)
    queries, own_block, own_kept = pl.pallas_call(
        projection_kernel,
        out_shape=[
            jax.ShapeDtypeStruct((head_count, row_count, head_dim), bf16),
            jax.ShapeDtypeStruct((row_count, head_dim), bf16),
            jax.ShapeDtypeStruct((row_count, head_dim), bf16),
        ],
        in_specs=[scalars] + whole(8),
        out_specs=whole(3),
        compiler_params=pltpu.CompilerParams(vmem_limit_bytes=32 * 2**20),
        name="projection",
    )(
        place,
        features,
        norm_gain[None, :],
        query_weight,
        kv_weight,
        query_bias[None, :],
        kv_bias[None, :],
        cosine,
        sine,
    )
    partner = lax.ppermute(own_block, "tp", [(i, i ^ 1) for i in range(group_count)])
    histories += [history(0), history(1)]
    chosen = first_pick(shared_owner, after(arrived, own_block, *histories), z_count)
    planes = lax.all_to_all(chosen, "z", 0, 0, tiled=True)
    slots[2] = after(slots[2], chosen)
    slots[3] = after(slots[3], chosen)
    histories += [history(2), history(3)]
    local = pl.pallas_call(
        functools.partial(local_kernel, chunk),
        out_shape=[
            jax.ShapeDtypeStruct((head_count, row_count, 2 * head_dim), f32),
            jax.ShapeDtypeStruct((head_count, row_count, head_dim), f32),
            jax.ShapeDtypeStruct((plane_count * node_total * chunk + row_count, head_dim), bf16),
        ],
        in_specs=[scalars] * 2 + whole(7),
        out_specs=whole(3),
        scratch_shapes=[pltpu.VMEM((row_count, head_dim), bf16)] * 2,
        compiler_params=pltpu.CompilerParams(vmem_limit_bytes=40 * 2**20),
        name="local",
    )(info, place, queries, own_kept, partner, *histories)
    kept = second_pick(shared_owner, after(planes, *local), plane_count, 1)[0]
    hot = lax.all_gather(kept, seq_axes[1:], axis=0, tiled=False)
    blocks = pl.pallas_call(
        shared_kernel,
        out_shape=jax.ShapeDtypeStruct((group_count, row_count, width), bf16),
        in_specs=whole(6),
        out_specs=whole(1)[0],
        compiler_params=pltpu.CompilerParams(vmem_limit_bytes=40 * 2**20),
        name="shared",
    )(queries, *local, hot, out_weight)
    summed = jnp.sum(lax.all_to_all(blocks, "tp", 0, 0, tiled=True).astype(f32), axis=0)
    hidden = (summed + tokens.astype(f32)).astype(bf16)
    return (hidden, own_block)


def solution(mesh):
    devices = mesh.devices
    split = Mesh(devices.reshape(8, devices.shape[0] // 16, 2, devices.shape[1]), seq_axes + ("tp",))
    by_seq = P(seq_axes, None)
    return jax.shard_map(
        on_device,
        mesh=split,
        in_specs=(
            P(seq_axes, "tp"),
            P(),
            P(None, "tp"),
            P("tp"),
            P(None, "tp"),
            P("tp"),
            P("tp", None),
            by_seq,
            P(),
            P(),
            P(seq_axes, None, None),
            by_seq,
            by_seq,
            by_seq,
            by_seq,
            by_seq,
        ),
        out_specs=(P(seq_axes, "tp"), P(seq_axes, "tp")),
        check_vma=False,
    )
```

```python
import functools
import math

import jax
import jax.numpy as jnp
from jax import lax
from jax.experimental import pallas as pl
from jax.experimental.pallas import tpu as pltpu
from jax.sharding import Mesh, PartitionSpec as P

norm_eps = 1e-06
rope_base = 1000000.0
neighbour_steps = (-2, -1, 1, 2)
seq_axes = ("z", "y", "core")
barred = -(2.0**100)
f32 = jnp.float32
bf16 = jnp.bfloat16
int32 = jnp.int32


def passed_along(block, axis, distance):
    devices = range(math.prod(lax.axis_size(name) for name in axis))
    return lax.ppermute(block, axis, [((i - distance) % len(devices), i) for i in devices])


def scalars_from(info_ref, requests):
    names = ("length", "depth", "slot", "parent")
    table = {
        name: [info_ref[n * requests + r] for r in range(requests)] for n, name in enumerate(names)
    }
    starts = [jnp.int32(0)]
    for r in range(requests - 1):
        starts.append(starts[r] + table["length"][r])
    table["start"] = starts
    return table


def by_request(index, starts, values):
    picked = jnp.full(index.shape, values[0], int32)
    for r in range(1, len(starts)):
        picked = jnp.where(index >= starts[r], values[r], picked)
    return picked


def prepare_kernel(
    info_ref, page_ref, place_ref, pool_ref, pos_ref, *rest
):
    outs, sems = rest[:-1], rest[-1]
    page_rows = pool_ref.shape[1]
    width = outs[0].shape[1]
    per_slot = outs[0].shape[0] // page_rows
    first = pl.multiple_of(place_ref[0] // 2 * width, width)
    copies = []
    for slot, out in enumerate(outs):
        for c in range(per_slot):
            n = slot * per_slot + c
            copies.append(
                pltpu.make_async_copy(
                    pool_ref.at[page_ref[n], :, pl.ds(first, width)],
                    out.at[pl.ds(c * page_rows, page_rows), :],
                    sems.at[n],
                )
            )
    for copy in copies:
        copy.start()
    requests = len(outs)
    table = scalars_from(info_ref, requests)
    base = []
    for r in range(requests):
        above = info_ref[4 * requests + 1 + table["parent"][r]]
        base.append(info_ref[4 * requests] + above + table["depth"][r] - table["start"][r])
    row = lax.broadcasted_iota(int32, pos_ref.shape, 0)
    pos_ref[...] = (row + by_request(row, table["start"], base)).astype(f32)
    for copy in copies:
        copy.wait()


def prepared(info, pages, place, hist_pool, row_count, slots, width):
    rows = pages.shape[0] // slots * hist_pool.shape[1]
    scalars = pl.BlockSpec(memory_space=pltpu.SMEM)
    anywhere = pl.BlockSpec(memory_space=pl.ANY)
    return pl.pallas_call(
        prepare_kernel,
        out_shape=[jax.ShapeDtypeStruct((row_count, width // 2), f32)]
        + [jax.ShapeDtypeStruct((rows, width), bf16)] * slots,
        in_specs=[scalars] * 3 + [anywhere],
        out_specs=whole(1 + slots),
        scratch_shapes=[pltpu.SemaphoreType.DMA((pages.shape[0],))],
        compiler_params=pltpu.CompilerParams(vmem_limit_bytes=4 * 2**20),
        name="prepare",
    )(info, pages, place, hist_pool)


def copied(tokens, count):
    def kernel(tok_ref, out_ref):
        for g in range(count):
            out_ref[g] = tok_ref[...]

    return pl.pallas_call(
        kernel,
        out_shape=jax.ShapeDtypeStruct((count,) + tokens.shape, bf16),
        in_specs=whole(1),
        out_specs=whole(1)[0],
        compiler_params=pltpu.CompilerParams(vmem_limit_bytes=4 * 2**20),
        name="copied",
    )(tokens)


def first_pick_kernel(owner_ref, arrived_ref, out_ref):
    per_plane = arrived_ref.shape[0]
    for n in range(out_ref.shape[1]):
        chosen = arrived_ref[lax.rem(owner_ref[n], per_plane)]
        for z in range(out_ref.shape[0]):
            out_ref[z, n] = chosen


def first_pick(owner, arrived, planes):
    return pl.pallas_call(
        first_pick_kernel,
        out_shape=jax.ShapeDtypeStruct((planes, owner.shape[0]) + arrived.shape[1:], bf16),
        in_specs=[pl.BlockSpec(memory_space=pltpu.SMEM)] + whole(1),
        out_specs=whole(1)[0],
        compiler_params=pltpu.CompilerParams(vmem_limit_bytes=4 * 2**20),
        name="first_pick",
    )(owner, arrived)


def second_pick(owner, planes, per_plane, copies):
    def kernel(owner_ref, planes_ref, out_ref):
        for n in range(out_ref.shape[1]):
            chosen = planes_ref[lax.div(owner_ref[n], per_plane), n]
            for c in range(copies):
                out_ref[c, n] = chosen

    return pl.pallas_call(
        kernel,
        out_shape=jax.ShapeDtypeStruct((copies,) + planes.shape[1:], bf16),
        in_specs=[pl.BlockSpec(memory_space=pltpu.SMEM)] + whole(1),
        out_specs=whole(1)[0],
        name="second_pick",
    )(owner, planes)


def projection_kernel(
    place_ref, tok_ref, gain_ref, wq_ref, wkv_ref, qb_ref, kb_ref, cos_ref, sin_ref,
    q_ref, own_ref, kept_ref
):
    groups, rows, width = tok_ref.shape
    total = jnp.zeros((rows, 1), f32)
    for g in range(groups):
        block = tok_ref[g].astype(f32)
        total = total + jnp.sum(block * block, axis=1, keepdims=True)
    inverse = lax.rsqrt(total / (groups * width) + norm_eps)
    query = jnp.zeros((rows, wq_ref.shape[1]), f32)
    fresh = jnp.zeros((rows, wkv_ref.shape[1]), f32)
    for g in range(groups):
        span = pl.ds(g * width, width)
        normed = (tok_ref[g].astype(f32) * inverse * gain_ref[:, span]).astype(bf16)
        query = query + jnp.dot(normed, wq_ref[span, :], preferred_element_type=f32)
        fresh = fresh + jnp.dot(normed, wkv_ref[span, :], preferred_element_type=f32)
    cosine = cos_ref[...]
    sine = sin_ref[...]
    half = cosine.shape[1] // 2

    def turned(part):
        return part * cosine + pltpu.roll(part, half, 1) * sine

    query = query + qb_ref[...]
    dim = cosine.shape[1]
    for h in range(q_ref.shape[0]):
        q_ref[h] = turned(query[:, h * dim : (h + 1) * dim]).astype(bf16)
    fresh = fresh + kb_ref[...]

    @pl.when(place_ref[0] % 2 == 0)
    def _():
        own_ref[...] = turned(fresh).astype(bf16)
        kept_ref[...] = turned(fresh).astype(bf16)

    @pl.when(place_ref[0] % 2 == 1)
    def _():
        own_ref[...] = fresh.astype(bf16)
        kept_ref[...] = fresh.astype(bf16)


def bars(bad):
    return jnp.where(bad, barred, 0.0).astype(bf16)


across = (((1,), (1,)), ((), ()))


def scale_of(dim):
    return dim ** (-0.5) * math.log2(math.e)


def local_kernel(
    chunk, info_ref, place_ref, q_ref, own_ref, partner_ref, h0_ref, h1_ref, h2_ref, h3_ref,
    mixed_ref, top_ref, bars_ref, key_ref, value_ref,
):
    heads, rows, dim = q_ref.shape
    hist_refs = (h0_ref, h1_ref, h2_ref, h3_ref)
    requests = len(hist_refs)
    table = scalars_from(info_ref, requests)
    starts, hist_len, slot, parent = (table[n] for n in ("start", "depth", "slot", "parent"))
    nodes = info_ref.shape[0] - 4 * requests
    shared_len = [info_ref[4 * requests + n] for n in range(nodes)]

    @pl.when(place_ref[0] % 2 == 0)
    def _():
        key_ref[...] = own_ref[...]
        value_ref[...] = partner_ref[...]

    @pl.when(place_ref[0] % 2 == 1)
    def _():
        key_ref[...] = partner_ref[...]
        value_ref[...] = own_ref[...]

    row = lax.broadcasted_iota(int32, (rows, dim), 0)
    lane = lax.broadcasted_iota(int32, (rows, dim), 1)
    hit = (
        (lane == by_request(row, starts, slot))
        | (lane == requests + by_request(row, starts, parent))
        | (lane == 2 * requests)
    )
    marks = jnp.where(hit, 1.0, 0.0).astype(bf16)
    shared_rows = bars_ref.shape[0] - rows
    bars_ref[shared_rows:, :] = marks

    per_chunk = chunk * nodes
    chunks = shared_rows // per_chunk
    index = lax.broadcasted_iota(int32, (per_chunk, dim), 0)
    side = lax.broadcasted_iota(int32, (per_chunk, dim), 1)
    node = jnp.zeros(index.shape, int32)
    left = jnp.full(index.shape, shared_len[0], int32)
    for n in range(1, nodes):
        node = jnp.where(index >= n * chunk, n, node)
        left = jnp.where(index >= n * chunk, shared_len[n], left)
    left = left - (index - node * chunk)
    other = (side >= requests) & (side < 2 * requests) & (node > 0) & (side != requests + node - 1)
    last = side == 2 * requests
    for s in range(chunks):
        bars_ref[s * per_chunk : (s + 1) * per_chunk, :] = bars(other | (last & (left <= s * chunk)))

    keys = []
    values = []
    for j in range(requests):
        deep = jnp.int32(0)
        for r in range(requests):
            deep = deep + jnp.where(slot[r] == j, hist_len[r], 0)
        place = lax.broadcasted_iota(int32, (hist_refs[j].shape[0], dim), 0)
        side = lax.broadcasted_iota(int32, (hist_refs[j].shape[0], dim), 1)
        bad = ((side < requests) & (side != j)) | ((side == 2 * requests) & (place >= deep))
        keys.append(jnp.concatenate([hist_refs[j][:, :dim], bars(bad)], axis=1))
        values.append(hist_refs[j][:, dim:])
    far_keys = jnp.concatenate(keys, axis=0)
    far_values = jnp.concatenate(values, axis=0)
    far_values = jnp.concatenate([far_values, jnp.ones_like(far_values)], axis=1)
    own_keys = key_ref[...]
    own_values = value_ref[...]
    own_values = jnp.concatenate([own_values, jnp.ones_like(own_values)], axis=1)

    wide_row = lax.broadcasted_iota(int32, (rows, rows), 0)
    wide_col = lax.broadcasted_iota(int32, (rows, rows), 1)
    numbers = list(range(requests))
    same = by_request(wide_row, starts, numbers) == by_request(wide_col, starts, numbers)
    unseen = jnp.where((wide_col <= wide_row) & same, 0.0, barred)

    scale = scale_of(dim)
    for h in range(heads):
        query = q_ref[h]
        far = lax.dot_general(
            jnp.concatenate([query, marks], axis=1), far_keys, across, preferred_element_type=f32
        )
        own = lax.dot_general(query, own_keys, across, preferred_element_type=f32) + unseen
        top = jnp.maximum(
            jnp.max(far, axis=1, keepdims=True), jnp.max(own, axis=1, keepdims=True)
        )
        far_weights = jnp.exp2((far - top) * scale).astype(bf16)
        own_weights = jnp.exp2((own - top) * scale).astype(bf16)
        mixed_ref[h] = jnp.dot(far_weights, far_values, preferred_element_type=f32) + jnp.dot(
            own_weights, own_values, preferred_element_type=f32
        )
        top_ref[h] = jnp.broadcast_to(top, (rows, dim))


def shared_kernel(q_ref, mixed_ref, top_ref, bars_ref, hot_ref, wo_ref, out_ref):
    heads, rows, dim = q_ref.shape
    chunks, nodes, chunk, _ = hot_ref.shape
    hot = hot_ref[...].reshape(chunks * nodes * chunk, 2 * dim)
    keys = jnp.concatenate([hot[:, :dim], bars_ref[: hot.shape[0], :]], axis=1)
    values = hot[:, dim:]
    values = jnp.concatenate([values, jnp.ones_like(values)], axis=1)
    marks = bars_ref[hot.shape[0] :, :]
    scale = scale_of(dim)
    merged = []
    for h in range(heads):
        scores = lax.dot_general(
            jnp.concatenate([q_ref[h], marks], axis=1), keys, across, preferred_element_type=f32
        )
        top = jnp.maximum(jnp.max(scores, axis=1, keepdims=True), top_ref[h][:, :1])
        weights = jnp.exp2((scores - top) * scale).astype(bf16)
        kept = jnp.exp2((top_ref[h] - top) * scale)
        local = mixed_ref[h]
        mixed = jnp.dot(weights, values, preferred_element_type=f32)
        total = mixed[:, dim:] + local[:, dim:] * kept
        merged.append(((mixed[:, :dim] + local[:, :dim] * kept) / total).astype(bf16))
    attention = jnp.concatenate(merged, axis=1)
    width = out_ref.shape[2]
    for g in range(out_ref.shape[0]):
        out_ref[g] = jnp.dot(
            attention, wo_ref[:, g * width : (g + 1) * width], preferred_element_type=f32
        ).astype(bf16)


def whole(count):
    return [pl.BlockSpec(memory_space=pltpu.VMEM)] * count


def on_device(
    tokens,
    norm_gain,
    query_weight,
    query_bias,
    kv_weight,
    kv_bias,
    out_weight,
    shared_slot,
    shared_len,
    shared_owner,
    hist_pool,
    hist_pages,
    hist_len,
    req_len,
    req_offset,
    req_parent,
):
    group_count = lax.axis_size("tp")
    row_count, width = tokens.shape
    head_dim = kv_bias.shape[0]
    head_count = query_weight.shape[1] // head_dim
    request_count = req_len.shape[1]
    tp_index = lax.axis_index("tp")
    place = jnp.stack([tp_index, lax.axis_index("core")]).astype(int32)
    scalars = pl.BlockSpec(memory_space=pltpu.SMEM)

    copies = copied(tokens, group_count)
    features = lax.all_to_all(copies, "tp", 0, 0, tiled=True)
    info = jnp.concatenate([req_len[0], hist_len[0], req_offset[0], req_parent[0], shared_len])
    position, *slots = prepared(
        info, hist_pages[0], place, hist_pool, row_count, request_count, 2 * head_dim
    )
    z_count, y_count, core_count = (lax.axis_size(name) for name in seq_axes)
    plane_count = y_count * core_count
    chunk = shared_slot.shape[0] // plane_count
    node_total = shared_owner.shape[0]

    def history(j):
        return passed_along(slots[j], seq_axes, -neighbour_steps[j])

    def after(value, *others):
        return lax.optimization_barrier((value, *others))[0]

    histories = []
    pieces = lax.dynamic_slice_in_dim(shared_slot, tp_index // 2 * 2 * head_dim, 2 * head_dim, 1)
    pieces = after(pieces, features, slots[3])
    arrived = lax.all_to_all(
        pieces.reshape(plane_count, chunk, -1), seq_axes[1:], 0, 0, tiled=True
    )

    half = head_dim // 2
    frequency = rope_base ** (-2.0 * jnp.arange(half, dtype=f32) / head_dim)
    angle = position[:, :half] * frequency[None, :]
    cosine = jnp.cos(angle)
    sine = jnp.sin(angle)
    cosine = jnp.concatenate([cosine, cosine], axis=1)
    sine = jnp.concatenate([-sine, sine], axis=1)
    queries, own_block, own_kept = pl.pallas_call(
        projection_kernel,
        out_shape=[
            jax.ShapeDtypeStruct((head_count, row_count, head_dim), bf16),
            jax.ShapeDtypeStruct((row_count, head_dim), bf16),
            jax.ShapeDtypeStruct((row_count, head_dim), bf16),
        ],
        in_specs=[scalars] + whole(8),
        out_specs=whole(3),
        compiler_params=pltpu.CompilerParams(vmem_limit_bytes=32 * 2**20),
        name="projection",
    )(
        place,
        features,
        norm_gain[None, :],
        query_weight,
        kv_weight,
        query_bias[None, :],
        kv_bias[None, :],
        cosine,
        sine,
    )
    partner = lax.ppermute(own_block, "tp", [(i, i ^ 1) for i in range(group_count)])
    histories += [history(0), history(1)]
    chosen = first_pick(shared_owner, after(arrived, own_block, *histories), z_count)
    planes = lax.all_to_all(chosen, "z", 0, 0, tiled=True)
    slots[2] = after(slots[2], chosen)
    slots[3] = after(slots[3], chosen)
    histories += [history(2), history(3)]
    local = pl.pallas_call(
        functools.partial(local_kernel, chunk),
        out_shape=[
            jax.ShapeDtypeStruct((head_count, row_count, 2 * head_dim), f32),
            jax.ShapeDtypeStruct((head_count, row_count, head_dim), f32),
            jax.ShapeDtypeStruct((plane_count * node_total * chunk + row_count, head_dim), bf16),
        ],
        in_specs=[scalars] * 2 + whole(7),
        out_specs=whole(3),
        scratch_shapes=[pltpu.VMEM((row_count, head_dim), bf16)] * 2,
        compiler_params=pltpu.CompilerParams(vmem_limit_bytes=40 * 2**20),
        name="local",
    )(info, place, queries, own_kept, partner, *histories)
    kept = second_pick(shared_owner, after(planes, *local), plane_count, 1)[0]
    hot = lax.all_gather(kept, seq_axes[1:], axis=0, tiled=False)
    blocks = pl.pallas_call(
        shared_kernel,
        out_shape=jax.ShapeDtypeStruct((group_count, row_count, width), bf16),
        in_specs=whole(6),
        out_specs=whole(1)[0],
        compiler_params=pltpu.CompilerParams(vmem_limit_bytes=40 * 2**20),
        name="shared",
    )(queries, *local, hot, out_weight)
    summed = jnp.sum(lax.all_to_all(blocks, "tp", 0, 0, tiled=True).astype(f32), axis=0)
    hidden = (summed + tokens.astype(f32)).astype(bf16)
    return (hidden, own_block)


def solution(mesh):
    devices = mesh.devices
    split = Mesh(devices.reshape(8, devices.shape[0] // 16, 2, devices.shape[1]), seq_axes + ("tp",))
    by_seq = P(seq_axes, None)
    return jax.shard_map(
        on_device,
        mesh=split,
        in_specs=(
            P(seq_axes, "tp"),
            P(),
            P(None, "tp"),
            P("tp"),
            P(None, "tp"),
            P("tp"),
            P("tp", None),
            by_seq,
            P(),
            P(),
            P(seq_axes, None, None),
            by_seq,
            by_seq,
            by_seq,
            by_seq,
            by_seq,
        ),
        out_specs=(P(seq_axes, "tp"), P(seq_axes, "tp")),
        check_vma=False,
    )
```
